32 devices in a mesh: segment: 4 (over x, core), dp: 4 (over z), tensor: 2 (over y).
Axes of the slice: x: 2, y: 2, z: 4, core: 2. Of those that a mesh axis runs over, the one named last changes fastest.
Arguments:
- acts: bfloat16 [4, 256, 1024], P('segment', ('dp', 'tensor')), may hold values from -6 to 6
- norm_gain: float32 [4, 1024], P('segment'), may hold values from 0.1 to 1.9
- final_gain: float32 [1024], replicated, may hold values from 0.1 to 1.9
- w_query: bfloat16 [4, 1024, 8192], P('segment', None, 'tensor'), may hold values from -0.015625 to 0.015625
- w_key: bfloat16 [4, 1024, 8192], P('segment', None, 'tensor'), may hold values from -0.1875 to 0.1875
- w_value: bfloat16 [4, 1024, 8192], P('segment', None, 'tensor'), may hold values from -0.1875 to 0.1875
- w_out: bfloat16 [4, 8192, 1024], P('segment', 'tensor'), may hold values from -0.0625 to 0.0625
- cache: bfloat16 [4, 2, 256, 8192], P('segment', None, 'dp', 'tensor'), may hold values from -6 to 6
Outputs:
- updated: bfloat16 [4, 256, 1024], P('segment', ('dp', 'tensor'))
- fresh: bfloat16 [4, 2, 256, 8192], P('segment', None, 'dp', 'tensor')
The draws below stay inside these ranges and needn't reach their ends.
All inputs are finite; a program needn't handle non-finite values.
Results may differ from the reference program's by a relative error of at most 0.01.
Values may be sent and summed in bfloat16 or wider, within the bound.
A program may use at most 64 MiB of HBM per device.

```python
import jax
import jax.numpy as jnp
from jax import lax

D = 1024
HDIM = 128
INNER = 8192
LEN = 64
ROWS = 256
ENC = 2
N_SEGMENT = 4
N_DP = 4
N_TENSOR = 2


def levels(stream_key, shape, shards, smallest, largest):
    factor_of = 1.0
    for position, shards_of in shards:
        draws = jax.random.uniform(jax.random.fold_in(jax.random.fold_in(stream_key, 6), position), (shards_of,), jnp.float32, smallest / len(shards), largest / len(shards))
        factor_of = factor_of * jnp.repeat(jnp.exp(draws), shape[position] // shards_of).reshape((-1,) + (1,) * (len(shape) - 1 - position))
    return factor_of


def scatter_about(key, shape, scale, limit, shards=(), dtype=jnp.bfloat16):
    level = levels(key, shape, shards, -0.22, 0.18) if shards else 1.0
    entries = jax.random.normal(key, shape, jnp.float32) * scale * level
    return jnp.minimum(jnp.maximum(entries, -limit), limit).astype(dtype)


def setup_inputs(seed: int = 0) -> dict:
    arg_keys = jax.random.split(jax.random.key(seed), 9)
    acts = scatter_about(arg_keys[0], (N_SEGMENT, ROWS, D), 1.0, 6.0, ((0, 4), (1, 8)))
    norm_gain = jnp.clip(1.0 + 0.18 * jax.random.normal(arg_keys[1], (N_SEGMENT, D), jnp.float32), 0.1, 1.9)
    final_gain = jnp.clip(1.0 + 0.18 * jax.random.normal(arg_keys[2], (D,), jnp.float32), 0.1, 1.9)
    w_query = scatter_about(arg_keys[3], (N_SEGMENT, D, INNER), (D * HDIM) ** -0.5, 0.015625, ((0, 4), (2, 2)))
    w_key = scatter_about(arg_keys[4], (N_SEGMENT, D, INNER), D ** -0.5, 0.1875, ((0, 4), (2, 2)))
    w_value = scatter_about(arg_keys[5], (N_SEGMENT, D, INNER), D ** -0.5, 0.1875, ((0, 4), (2, 2)))
    w_out = scatter_about(arg_keys[6], (N_SEGMENT, INNER, D), INNER ** -0.5, 0.0625, ((0, 4), (1, 2)))
    cache = scatter_about(arg_keys[7], (N_SEGMENT, 2, ROWS, INNER), 1.0, 6.0, ((0, 4), (2, 4), (3, 2)))
    return dict(acts=acts, norm_gain=norm_gain, final_gain=final_gain, w_query=w_query, w_key=w_key, w_value=w_value, w_out=w_out, cache=cache)


EPSILON = 1e-06

def normalize(values, gain):
    wide = values.astype(jnp.float32)
    scale = lax.rsqrt(lax.optimization_barrier(jnp.mean(wide * wide, axis=-1, keepdims=True)) + EPSILON)
    return (wide * scale * gain.astype(jnp.float32)).astype(jnp.bfloat16)

def attend(queries, keys, values):
    length = queries.shape[0]
    heads = queries.shape[1] // HDIM
    query_heads = queries.reshape(length, heads, HDIM).astype(jnp.float32)
    key_heads = keys.reshape(keys.shape[0], heads, HDIM).astype(jnp.float32)
    value_heads = values.reshape(values.shape[0], heads, HDIM).astype(jnp.float32)
    scores = jnp.einsum('qhd,khd->hqk', query_heads, key_heads)
    weights = jnp.exp(scores)
    probs = (weights / lax.optimization_barrier(jnp.sum(weights, axis=-1, keepdims=True))).astype(jnp.bfloat16)
    context = jnp.einsum('hqk,khd->qhd', probs.astype(jnp.float32), value_heads)
    return context.reshape(length, heads * HDIM).astype(jnp.bfloat16)

def section(tokens, gain, w_query, w_key, w_value, w_out, cache, memory, decoder):
    normed = normalize(tokens, gain)
    queries = jnp.dot(normed, w_query, preferred_element_type=jnp.float32).astype(jnp.bfloat16)
    own_keys = jnp.dot(normed, w_key, preferred_element_type=jnp.float32).astype(jnp.bfloat16)
    own_values = jnp.dot(normed, w_value, preferred_element_type=jnp.float32).astype(jnp.bfloat16)
    keys = jnp.where(decoder, cache[0], own_keys)
    values = jnp.where(decoder, cache[1], own_values)
    inner = queries.shape[1]
    trio = (queries.reshape(N_DP, LEN, inner), keys.reshape(N_DP, LEN, inner), values.reshape(N_DP, LEN, inner))
    context = lax.map(lambda item: attend(item[0], item[1], item[2]), trio).reshape(ROWS, inner)
    group = inner // N_TENSOR
    context_groups = jnp.transpose(context.reshape(ROWS, N_TENSOR, group), (1, 0, 2))
    weight_groups = w_out.reshape(N_TENSOR, group, D)

    def group_term(pair):
        rounded = jnp.dot(pair[0], pair[1], preferred_element_type=jnp.float32).astype(jnp.bfloat16)
        rounded = lax.optimization_barrier(rounded)
        return rounded.astype(jnp.float32)
    partials = lax.map(group_term, (context_groups, weight_groups))
    branch = lax.optimization_barrier(jnp.sum(partials, axis=0))
    updated = (tokens.astype(jnp.float32) + branch).astype(jnp.bfloat16)
    memory_keys = jnp.dot(memory, w_key, preferred_element_type=jnp.float32).astype(jnp.bfloat16)
    memory_values = jnp.dot(memory, w_value, preferred_element_type=jnp.float32).astype(jnp.bfloat16)
    fresh = jnp.where(decoder, jnp.stack([memory_keys, memory_values]), jnp.stack([own_keys, own_values]))
    return (updated, fresh)

def reference(acts, norm_gain, final_gain, w_query, w_key, w_value, w_out, cache):
    root = ENC - 1
    blank = jnp.zeros((ROWS, D), jnp.bfloat16)
    root_updated, unused = section(acts[root], norm_gain[root], w_query[root], w_key[root], w_value[root], w_out[root], cache[root], blank, False)
    memory = normalize(root_updated, final_gain)
    indices = jnp.arange(N_SEGMENT).astype(jnp.int32)

    def one_section(item):
        return section(item[0], item[1], item[2], item[3], item[4], item[5], item[6], memory, item[7] >= ENC)
    updated, fresh = lax.map(one_section, (acts, norm_gain, w_query, w_key, w_value, w_out, cache, indices))
    return (updated, fresh)
```

```python
import functools

import jax
import jax.numpy as jnp
from jax import lax
from jax.experimental import pallas as pl
from jax.experimental.pallas import tpu as pltpu
from jax.sharding import PartitionSpec as P

HDIM = 128
EPSILON = 1e-06
MESH = pl.DeviceIdType.MESH
F32 = jnp.float32
BF16 = jnp.bfloat16


def largest(total, limit):
    width = min(total, limit)
    while total % width:
        width -= HDIM
    return width


def kernel(
    sections, split, wide, narrow,
    acts, norm_gain, final_gain, w_query, w_key, w_value, w_out, cache,
    updated, fresh,
    query_buf, key_buf, value_buf, out_buf, cache_buf, gain_buf, final_buf,
    gathered, normed, context, own_part, got_part, sent_rows, got_rows, total,
    qkv_sem, out_sem, small_sem, act_send, act_recv, part_send, part_recv, mem_send, mem_recv,
):
    segment = lax.axis_index("segment")
    me = lax.axis_index("tensor")
    half = sections // 2
    root = half - 1
    decoder = segment >= half
    encoder = segment < half
    is_root = segment == root
    not_root = segment != root
    parts, local_rows, features = gathered.shape
    rows = parts * local_rows
    groups = query_buf.shape[0]
    blocks = out_buf.shape[0]

    def columns(j):
        return pl.ds(pl.multiple_of(j * wide, wide), wide)

    def load_qkv(which, source, target, j):
        return pltpu.make_async_copy(source.at[0, :, columns(j)], target.at[j], qkv_sem.at[which, j])

    def load_q(j):
        return load_qkv(0, w_query, query_buf, j)

    def load_k(j):
        return load_qkv(1, w_key, key_buf, j)

    def load_v(j):
        return load_qkv(2, w_value, value_buf, j)

    def load_out(c):
        return pltpu.make_async_copy(w_out.at[0, :, pl.ds(c * narrow, narrow)], out_buf.at[c], out_sem.at[c])

    own_acts = pltpu.make_async_copy(acts.at[0], gathered.at[me], small_sem.at[0])
    gain_copy = pltpu.make_async_copy(norm_gain, gain_buf, small_sem.at[1])
    final_copy = pltpu.make_async_copy(final_gain, final_buf, small_sem.at[2])
    cache_copy = pltpu.make_async_copy(cache.at[0], cache_buf, small_sem.at[3])

    barrier = pltpu.get_barrier_semaphore()
    for off in range(1, split):
        pl.semaphore_signal(barrier, inc=1, device_id={"tensor": lax.rem(me + off, split)}, device_id_type=MESH)

    @pl.when(is_root)
    def _():
        for s in range(half, sections):
            pl.semaphore_signal(barrier, inc=1, device_id={"segment": s}, device_id_type=MESH)

    @pl.when(decoder)
    def _():
        pl.semaphore_signal(barrier, inc=1, device_id={"segment": root}, device_id_type=MESH)

    own_acts.start()
    gain_copy.start()
    final_copy.start()

    @pl.when(encoder)
    def _():
        def begin(j, carry):
            load_q(j).start()
            load_k(j).start()
            load_v(j).start()
            return carry

        lax.fori_loop(0, groups, begin, 0)
        for c in range(blocks):
            load_out(c).start()

    @pl.when(decoder)
    def _():
        cache_copy.start()

        def begin(j, carry):
            load_q(j).start()
            return carry

        lax.fori_loop(0, groups, begin, 0)
        for c in range(blocks):
            load_out(c).start()

        def begin_pair(j, carry):
            load_k(j).start()
            load_v(j).start()
            return carry

        lax.fori_loop(0, groups, begin_pair, 0)

    @pl.when(is_root)
    def _():
        pl.semaphore_wait(barrier, split - 1 + sections - half)

    @pl.when(decoder)
    def _():
        pl.semaphore_wait(barrier, split)

    @pl.when(encoder & not_root)
    def _():
        pl.semaphore_wait(barrier, split - 1)

    def send_acts(off):
        return pltpu.make_async_remote_copy(
            src_ref=acts.at[0],
            dst_ref=gathered.at[me],
            send_sem=act_send.at[off - 1],
            recv_sem=act_recv.at[off - 1],
            device_id={"tensor": lax.rem(me + off, split)},
            device_id_type=MESH,
        )

    def send_all_rows(off, c):
        return pltpu.make_async_remote_copy(
            src_ref=own_part.at[c],
            dst_ref=got_part.at[off - 1, c],
            send_sem=part_send.at[off - 1, c],
            recv_sem=part_recv.at[off - 1, c],
            device_id={"tensor": lax.rem(me + off, split)},
            device_id_type=MESH,
        )

    def send_their_rows(off, c):
        peer = lax.rem(me + off, split)
        return pltpu.make_async_remote_copy(
            src_ref=own_part.at[c, peer],
            dst_ref=got_part.at[off - 1, c, peer],
            send_sem=part_send.at[off - 1, c],
            recv_sem=part_recv.at[off - 1, c],
            device_id={"tensor": peer},
            device_id_type=MESH,
        )

    def send_memory(s, c):
        return pltpu.make_async_remote_copy(
            src_ref=sent_rows.at[c],
            dst_ref=got_rows.at[c],
            send_sem=mem_send.at[s - half, c],
            recv_sem=mem_recv.at[c],
            device_id={"segment": s},
            device_id_type=MESH,
        )

    for off in range(1, split):
        send_acts(off).start()
    own_acts.wait()
    gain_copy.wait()
    final_copy.wait()
    for off in range(1, split):
        send_acts(off).wait_recv()

    tokens = gathered[...].reshape(rows, features).astype(F32)
    scale = lax.rsqrt(jnp.mean(tokens * tokens, axis=-1, keepdims=True) + EPSILON)
    normed[...] = (tokens * scale * gain_buf[...]).astype(BF16)

    def attend(queries, keys, values):
        results = []
        for h in range(wide // HDIM):
            cols = slice(h * HDIM, (h + 1) * HDIM)
            scores = lax.dot_general(
                queries[:, cols], keys[:, cols], (((1,), (1,)), ((), ())), preferred_element_type=F32
            )
            weights = jnp.exp(scores)
            probs = (weights / jnp.sum(weights, axis=-1, keepdims=True)).astype(BF16)
            results.append(jnp.dot(probs, values[:, cols], preferred_element_type=F32).astype(BF16))
        return jnp.concatenate(results, axis=1)

    @pl.when(encoder)
    def _():
        def group(j, carry):
            source = normed[...]
            load_q(j).wait()
            queries = jnp.dot(source, query_buf[j], preferred_element_type=F32).astype(BF16)
            load_k(j).wait()
            keys = jnp.dot(source, key_buf[j], preferred_element_type=F32).astype(BF16)
            load_v(j).wait()
            values = jnp.dot(source, value_buf[j], preferred_element_type=F32).astype(BF16)
            fresh[0, 0, :, columns(j)] = keys
            fresh[0, 1, :, columns(j)] = values
            context[:, columns(j)] = attend(queries, keys, values)
            return carry

        lax.fori_loop(0, groups, group, 0)

    @pl.when(decoder)
    def _():
        cache_copy.wait()

        def group(j, carry):
            load_q(j).wait()
            queries = jnp.dot(normed[...], query_buf[j], preferred_element_type=F32).astype(BF16)
            context[:, columns(j)] = attend(queries, cache_buf[0, :, columns(j)], cache_buf[1, :, columns(j)])
            return carry

        lax.fori_loop(0, groups, group, 0)

    def project(c):
        load_out(c).wait()
        made = jnp.dot(context[...], out_buf[c], preferred_element_type=F32).astype(BF16)
        own_part[c] = made.reshape(parts, local_rows, narrow)

        @pl.when(is_root)
        def _():
            for off in range(1, split):
                send_all_rows(off, c).start()

        @pl.when(not_root)
        def _():
            for off in range(1, split):
                send_their_rows(off, c).start()

    def combine(c):
        cols = slice(c * narrow, (c + 1) * narrow)

        @pl.when(is_root)
        def _():
            for off in range(1, split):
                send_all_rows(off, c).wait_recv()
            branch = own_part[c].astype(F32)
            for off in range(1, split):
                branch = branch + got_part[off - 1, c].astype(F32)
            sent_rows[c] = (gathered[:, :, cols].astype(F32) + branch).astype(BF16)
            for s in range(half, sections):
                send_memory(s, c).start()
            updated[0, :, cols] = sent_rows[c, me]

        @pl.when(not_root)
        def _():
            for off in range(1, split):
                send_their_rows(off, c).wait_recv()
            branch = own_part[c, me].astype(F32)
            for off in range(1, split):
                branch = branch + got_part[off - 1, c, me].astype(F32)
            updated[0, :, cols] = (gathered[me, :, cols].astype(F32) + branch).astype(BF16)

    lag = min(2, blocks - 1)
    for c in range(blocks):
        project(c)
        if c >= lag:
            combine(c - lag)
    for c in range(blocks - lag, blocks):
        combine(c)

    @pl.when(decoder)
    def _():
        def arrive(j, carry):
            load_k(j).wait()
            load_v(j).wait()
            return carry

        lax.fori_loop(0, groups, arrive, 0)
        squares = jnp.zeros((rows, 1), F32)
        for c in range(blocks):
            cols = slice(c * narrow, (c + 1) * narrow)
            send_memory(half, c).wait_recv()
            memory = got_rows[c].reshape(rows, narrow).astype(F32)
            squares = squares + jnp.sum(memory * memory, axis=-1, keepdims=True)
            source = (memory * final_buf[:, cols]).astype(BF16)
            last = c == blocks - 1
            if last:
                scale = lax.rsqrt(squares * (1.0 / features) + EPSILON)

            def group(j, carry):
                for which, weights in ((0, key_buf), (1, value_buf)):
                    term = jnp.dot(source, weights[j, cols, :], preferred_element_type=F32)
                    if c > 0:
                        term = term + total[which, j]
                    if last:
                        fresh[0, which, :, columns(j)] = (term * scale).astype(BF16)
                    else:
                        total[which, j] = term
                return carry

            lax.fori_loop(0, groups, group, 0)

    for off in range(1, split):
        send_acts(off).wait_send()

    @pl.when(is_root)
    def _():
        for c in range(blocks):
            for off in range(1, split):
                send_all_rows(off, c).wait_send()
            for s in range(half, sections):
                send_memory(s, c).wait_send()

    @pl.when(not_root)
    def _():
        for c in range(blocks):
            for off in range(1, split):
                send_their_rows(off, c).wait_send()


def solution(mesh):
    sections, split = mesh.shape["segment"], mesh.shape["tensor"]

    def on_device(acts, norm_gain, final_gain, w_query, w_key, w_value, w_out, cache):
        local_rows, features = acts.shape[1:]
        inner = w_query.shape[2]
        rows = split * local_rows
        wide = largest(inner, 512)
        narrow = largest(features, 256)
        groups, blocks = inner // wide, features // narrow
        dma = pltpu.SemaphoreType.DMA
        return pl.pallas_call(
            functools.partial(kernel, sections, split, wide, narrow),
            out_shape=(
                jax.ShapeDtypeStruct(acts.shape, BF16),
                jax.ShapeDtypeStruct(cache.shape, BF16),
            ),
            in_specs=[pl.BlockSpec(memory_space=pltpu.HBM)] * 8,
            out_specs=(pl.BlockSpec(memory_space=pltpu.VMEM), pl.BlockSpec(memory_space=pltpu.VMEM)),
            scratch_shapes=[
                pltpu.VMEM((groups, features, wide), BF16),
                pltpu.VMEM((groups, features, wide), BF16),
                pltpu.VMEM((groups, features, wide), BF16),
                pltpu.VMEM((blocks, inner, narrow), BF16),
                pltpu.VMEM((2, rows, inner), BF16),
                pltpu.VMEM((1, features), F32),
                pltpu.VMEM((1, features), F32),
                pltpu.VMEM((split, local_rows, features), BF16),
                pltpu.VMEM((rows, features), BF16),
                pltpu.VMEM((rows, inner), BF16),
                pltpu.VMEM((blocks, split, local_rows, narrow), BF16),
                pltpu.VMEM((split - 1, blocks, split, local_rows, narrow), BF16),
                pltpu.VMEM((blocks, split, local_rows, narrow), BF16),
                pltpu.VMEM((blocks, split, local_rows, narrow), BF16),
                pltpu.VMEM((2, groups, rows, wide), F32),
                dma((3, groups)),
                dma((blocks,)),
                dma((4,)),
                dma((split - 1,)),
                dma((split - 1,)),
                dma((split - 1, blocks)),
                dma((split - 1, blocks)),
                dma((sections - sections // 2, blocks)),
                dma((blocks,)),
            ],
            compiler_params=pltpu.CompilerParams(
                collective_id=0, has_side_effects=True, vmem_limit_bytes=58 * 1024 * 1024
            ),
        )(acts, norm_gain, final_gain.reshape(1, features), w_query, w_key, w_value, w_out, cache)

    placed = (
        P("segment", ("dp", "tensor"), None),
        P("segment", None),
        P(),
        P("segment", None, "tensor"),
        P("segment", None, "tensor"),
        P("segment", None, "tensor"),
        P("segment", "tensor", None),
        P("segment", None, "dp", "tensor"),
    )
    return jax.shard_map(
        on_device,
        mesh=mesh,
        in_specs=placed,
        out_specs=(P("segment", ("dp", "tensor"), None), P("segment", None, "dp", "tensor")),
        check_vma=False,
    )
```

```python
import functools

import jax
import jax.numpy as jnp
from jax import lax
from jax.experimental import pallas as pl
from jax.experimental.pallas import tpu as pltpu
from jax.sharding import PartitionSpec as P

HDIM = 128
EPSILON = 1e-06
MESH = pl.DeviceIdType.MESH
F32 = jnp.float32
BF16 = jnp.bfloat16
LARGEST = float(jnp.finfo(jnp.bfloat16).max)


def largest(total, limit):
    width = min(total, limit)
    while total % width:
        width -= HDIM
    return width


def kernel(
    sections, split, wide, narrow,
    acts, norm_gain, final_gain, w_query, w_key, w_value, w_out, cache,
    updated, fresh,
    query_buf, key_buf, value_buf, out_buf, cache_buf, gain_buf, final_buf,
    gathered, normed, context, own_part, got_part, sent_rows, got_rows, total, slots, same_head,
    qkv_sem, out_sem, small_sem, act_send, act_recv, part_send, part_recv, mem_send, mem_recv,
):
    segment = lax.axis_index("segment")
    me = lax.axis_index("tensor")
    half = sections // 2
    root = half - 1
    decoder = segment >= half
    encoder = segment < half
    is_root = segment == root
    not_root = segment != root
    parts, local_rows, features = gathered.shape
    rows = parts * local_rows
    groups = query_buf.shape[0]
    blocks = out_buf.shape[0]

    def columns(j):
        return pl.ds(pl.multiple_of(j * wide, wide), wide)

    def load_qkv(which, source, target, j):
        return pltpu.make_async_copy(source.at[0, :, columns(j)], target.at[j], qkv_sem.at[which, j])

    def load_q(j):
        return load_qkv(0, w_query, query_buf, j)

    def load_k(j):
        return load_qkv(1, w_key, key_buf, j)

    def load_v(j):
        return load_qkv(2, w_value, value_buf, j)

    def load_out(c):
        return pltpu.make_async_copy(w_out.at[0, :, pl.ds(c * narrow, narrow)], out_buf.at[c], out_sem.at[c])

    own_acts = pltpu.make_async_copy(acts.at[0], gathered.at[me], small_sem.at[0])
    gain_copy = pltpu.make_async_copy(norm_gain, gain_buf, small_sem.at[1])
    final_copy = pltpu.make_async_copy(final_gain, final_buf, small_sem.at[2])
    cache_copy = pltpu.make_async_copy(cache.at[0], cache_buf, small_sem.at[3])

    barrier = pltpu.get_barrier_semaphore()
    for off in range(1, split):
        pl.semaphore_signal(barrier, inc=1, device_id={"tensor": lax.rem(me + off, split)}, device_id_type=MESH)

    @pl.when(is_root)
    def _():
        for s in range(half, sections):
            pl.semaphore_signal(barrier, inc=1, device_id={"segment": s}, device_id_type=MESH)

    @pl.when(decoder)
    def _():
        pl.semaphore_signal(barrier, inc=1, device_id={"segment": root}, device_id_type=MESH)

    own_acts.start()
    gain_copy.start()
    final_copy.start()

    @pl.when(encoder)
    def _():
        def begin(j, carry):
            load_q(j).start()
            load_k(j).start()
            load_v(j).start()
            return carry

        lax.fori_loop(0, groups, begin, 0)
        for c in range(blocks):
            load_out(c).start()

    @pl.when(decoder)
    def _():
        cache_copy.start()

        def begin(j, carry):
            load_q(j).start()
            return carry

        lax.fori_loop(0, groups, begin, 0)
        for c in range(blocks):
            load_out(c).start()

        def begin_pair(j, carry):
            load_k(j).start()
            load_v(j).start()
            return carry

        lax.fori_loop(0, groups, begin_pair, 0)

    @pl.when(is_root)
    def _():
        pl.semaphore_wait(barrier, split - 1 + sections - half)

    @pl.when(decoder)
    def _():
        pl.semaphore_wait(barrier, split)

    @pl.when(encoder & not_root)
    def _():
        pl.semaphore_wait(barrier, split - 1)

    def send_acts(off):
        return pltpu.make_async_remote_copy(
            src_ref=acts.at[0],
            dst_ref=gathered.at[me],
            send_sem=act_send.at[off - 1],
            recv_sem=act_recv.at[off - 1],
            device_id={"tensor": lax.rem(me + off, split)},
            device_id_type=MESH,
        )

    def send_all_rows(off, c):
        return pltpu.make_async_remote_copy(
            src_ref=own_part.at[c],
            dst_ref=got_part.at[off - 1, c],
            send_sem=part_send.at[off - 1, c],
            recv_sem=part_recv.at[off - 1, c],
            device_id={"tensor": lax.rem(me + off, split)},
            device_id_type=MESH,
        )

    def send_their_rows(off, c):
        peer = lax.rem(me + off, split)
        return pltpu.make_async_remote_copy(
            src_ref=own_part.at[c, peer],
            dst_ref=got_part.at[off - 1, c, peer],
            send_sem=part_send.at[off - 1, c],
            recv_sem=part_recv.at[off - 1, c],
            device_id={"tensor": peer},
            device_id_type=MESH,
        )

    def send_memory(s, c):
        return pltpu.make_async_remote_copy(
            src_ref=sent_rows.at[c],
            dst_ref=got_rows.at[c],
            send_sem=mem_send.at[s - half, c],
            recv_sem=mem_recv.at[c],
            device_id={"segment": s},
            device_id_type=MESH,
        )

    for off in range(1, split):
        send_acts(off).start()
    own_acts.wait()
    gain_copy.wait()
    final_copy.wait()
    for off in range(1, split):
        send_acts(off).wait_recv()

    tokens = gathered[...].reshape(rows, features).astype(F32)
    scale = lax.rsqrt(jnp.mean(tokens * tokens, axis=-1, keepdims=True) + EPSILON)
    normed[...] = (tokens * scale * gain_buf[...]).astype(BF16)

    which_row = lax.broadcasted_iota(jnp.int32, same_head.shape, 0) < rows
    which_column = lax.broadcasted_iota(jnp.int32, same_head.shape, 1) < rows
    same_head[...] = jnp.where(which_row == which_column, 1.0, 0.0).astype(BF16)

    def attend(queries, keys, values):
        blank = jnp.zeros((rows, HDIM), BF16)
        pairs = wide // (2 * HDIM)

        def spread(source, p):
            first = source[:, 2 * p * HDIM : (2 * p + 1) * HDIM]
            second = source[:, (2 * p + 1) * HDIM : (2 * p + 2) * HDIM]
            return jnp.concatenate(
                [jnp.concatenate([first, blank], axis=1), jnp.concatenate([blank, second], axis=1)], axis=0
            )

        scores = [
            lax.dot_general(
                queries[:, 2 * p * HDIM : (2 * p + 2) * HDIM], spread(keys, p),
                (((1,), (1,)), ((), ())), preferred_element_type=F32,
            )
            for p in range(pairs)
        ]
        weights = [jnp.minimum(jnp.exp(score), LARGEST) for score in scores]
        ones = same_head[...]
        sums = [jnp.dot(weight.astype(BF16), ones, preferred_element_type=F32) for weight in weights]
        probs = [(weight / total_of).astype(BF16) for weight, total_of in zip(weights, sums)]
        results = [
            jnp.dot(probs[p], spread(values, p), preferred_element_type=F32).astype(BF16) for p in range(pairs)
        ]
        return jnp.concatenate(results, axis=1)

    def attend_slot(slot, j):
        context[:, columns(j)] = attend(slots[slot, 0], slots[slot, 1], slots[slot, 2])

    def own_group(slot, j):
        source = normed[...]
        for which, weights in ((0, query_buf), (1, key_buf), (2, value_buf)):
            made = jnp.dot(source, weights[j], preferred_element_type=F32).astype(BF16)
            slots[slot, which] = made
            if which > 0:
                fresh[0, which - 1, :, columns(j)] = made

    def cached_group(slot, j):
        made = jnp.dot(normed[...], query_buf[j], preferred_element_type=F32).astype(BF16)
        slots[slot, 0] = made
        slots[slot, 1] = cache_buf[0, :, columns(j)]
        slots[slot, 2] = cache_buf[1, :, columns(j)]

    def pipelined(wait, make):
        wait(0)
        make(0, 0)

        def pair(i, carry):
            j = 2 * i + 1
            wait(j)
            attend_slot(0, j - 1)
            make(1, j)
            wait(j + 1)
            attend_slot(1, j)
            make(0, j + 1)
            return carry

        lax.fori_loop(0, (groups - 1) // 2, pair, 0)
        if groups % 2 == 0:
            wait(groups - 1)
            attend_slot(0, groups - 2)
            make(1, groups - 1)
        attend_slot((groups - 1) % 2, groups - 1)

    @pl.when(encoder)
    def _():
        def wait(j):
            load_q(j).wait()
            load_k(j).wait()
            load_v(j).wait()

        pipelined(wait, own_group)

    @pl.when(decoder)
    def _():
        cache_copy.wait()
        pipelined(lambda j: load_q(j).wait(), cached_group)

    def project(c):
        load_out(c).wait()
        made = jnp.dot(context[...], out_buf[c], preferred_element_type=F32).astype(BF16)
        own_part[c] = made.reshape(parts, local_rows, narrow)

        @pl.when(is_root)
        def _():
            for off in range(1, split):
                send_all_rows(off, c).start()

        @pl.when(not_root)
        def _():
            for off in range(1, split):
                send_their_rows(off, c).start()

    def combine(c):
        cols = slice(c * narrow, (c + 1) * narrow)

        @pl.when(is_root)
        def _():
            for off in range(1, split):
                send_all_rows(off, c).wait_recv()
            branch = own_part[c].astype(F32)
            for off in range(1, split):
                branch = branch + got_part[off - 1, c].astype(F32)
            sent_rows[c] = (gathered[:, :, cols].astype(F32) + branch).astype(BF16)
            for s in range(half, sections):
                send_memory(s, c).start()
            updated[0, :, cols] = sent_rows[c, me]

        @pl.when(not_root)
        def _():
            for off in range(1, split):
                send_their_rows(off, c).wait_recv()
            branch = own_part[c, me].astype(F32)
            for off in range(1, split):
                branch = branch + got_part[off - 1, c, me].astype(F32)
            updated[0, :, cols] = (gathered[me, :, cols].astype(F32) + branch).astype(BF16)

    lag = min(2, blocks - 1)
    for c in range(blocks):
        project(c)
        if c >= lag:
            combine(c - lag)
    for c in range(blocks - lag, blocks):
        combine(c)

    @pl.when(decoder)
    def _():
        def arrive(j, carry):
            load_k(j).wait()
            load_v(j).wait()
            return carry

        lax.fori_loop(0, groups, arrive, 0)
        squares = jnp.zeros((rows, 1), F32)
        for c in range(blocks):
            cols = slice(c * narrow, (c + 1) * narrow)
            send_memory(half, c).wait_recv()
            memory = got_rows[c].reshape(rows, narrow).astype(F32)
            squares = squares + jnp.sum(memory * memory, axis=-1, keepdims=True)
            source = (memory * final_buf[:, cols]).astype(BF16)
            last = c == blocks - 1
            if last:
                scale = lax.rsqrt(squares * (1.0 / features) + EPSILON)

            def group(j, carry):
                for which, weights in ((0, key_buf), (1, value_buf)):
                    term = jnp.dot(source, weights[j, cols, :], preferred_element_type=F32)
                    if c > 0:
                        term = term + total[which, j]
                    if last:
                        fresh[0, which, :, columns(j)] = (term * scale).astype(BF16)
                    else:
                        total[which, j] = term
                return carry

            lax.fori_loop(0, groups, group, 0)

    for off in range(1, split):
        send_acts(off).wait_send()

    @pl.when(is_root)
    def _():
        for c in range(blocks):
            for off in range(1, split):
                send_all_rows(off, c).wait_send()
            for s in range(half, sections):
                send_memory(s, c).wait_send()

    @pl.when(not_root)
    def _():
        for c in range(blocks):
            for off in range(1, split):
                send_their_rows(off, c).wait_send()


def solution(mesh):
    sections, split = mesh.shape["segment"], mesh.shape["tensor"]

    def on_device(acts, norm_gain, final_gain, w_query, w_key, w_value, w_out, cache):
        local_rows, features = acts.shape[1:]
        inner = w_query.shape[2]
        rows = split * local_rows
        wide = largest(inner, 1024)
        narrow = largest(features, 256)
        groups, blocks = inner // wide, features // narrow
        dma = pltpu.SemaphoreType.DMA
        return pl.pallas_call(
            functools.partial(kernel, sections, split, wide, narrow),
            out_shape=(pltpu.VMEM(acts.shape, BF16), pltpu.VMEM(cache.shape, BF16)),
            in_specs=[pl.BlockSpec(memory_space=pltpu.HBM)] * 8,
            out_specs=(pl.BlockSpec(memory_space=pltpu.VMEM), pl.BlockSpec(memory_space=pltpu.VMEM)),
            scratch_shapes=[
                pltpu.VMEM((groups, features, wide), BF16),
                pltpu.VMEM((groups, features, wide), BF16),
                pltpu.VMEM((groups, features, wide), BF16),
                pltpu.VMEM((blocks, inner, narrow), BF16),
                pltpu.VMEM((2, rows, inner), BF16),
                pltpu.VMEM((1, features), F32),
                pltpu.VMEM((1, features), F32),
                pltpu.VMEM((split, local_rows, features), BF16),
                pltpu.VMEM((rows, features), BF16),
                pltpu.VMEM((rows, inner), BF16),
                pltpu.VMEM((blocks, split, local_rows, narrow), BF16),
                pltpu.VMEM((split - 1, blocks, split, local_rows, narrow), BF16),
                pltpu.VMEM((blocks, split, local_rows, narrow), BF16),
                pltpu.VMEM((blocks, split, local_rows, narrow), BF16),
                pltpu.VMEM((2, groups, rows, wide), F32),
                pltpu.VMEM((2, 3, rows, wide), BF16),
                pltpu.VMEM((2 * rows, 2 * rows), BF16),
                dma((3, groups)),
                dma((blocks,)),
                dma((4,)),
                dma((split - 1,)),
                dma((split - 1,)),
                dma((split - 1, blocks)),
                dma((split - 1, blocks)),
                dma((sections - sections // 2, blocks)),
                dma((blocks,)),
            ],
            compiler_params=pltpu.CompilerParams(
                collective_id=0, has_side_effects=True, vmem_limit_bytes=58 * 1024 * 1024
            ),
        )(acts, norm_gain, final_gain.reshape(1, features), w_query, w_key, w_value, w_out, cache)

    placed = (
        P("segment", ("dp", "tensor"), None),
        P("segment", None),
        P(),
        P("segment", None, "tensor"),
        P("segment", None, "tensor"),
        P("segment", None, "tensor"),
        P("segment", "tensor", None),
        P("segment", None, "dp", "tensor"),
    )
    return jax.shard_map(
        on_device,
        mesh=mesh,
        in_specs=placed,
        out_specs=(P("segment", ("dp", "tensor"), None), P("segment", None, "dp", "tensor")),
        check_vma=False,
    )
```

```python
import functools

import jax
import jax.numpy as jnp
from jax import lax
from jax.experimental import pallas as pl
from jax.experimental.pallas import tpu as pltpu
from jax.sharding import PartitionSpec as P

HDIM = 128
EPSILON = 1e-06
MESH = pl.DeviceIdType.MESH
F32 = jnp.float32
BF16 = jnp.bfloat16
LARGEST = float(jnp.finfo(jnp.bfloat16).max)


def largest(total, limit):
    width = min(total, limit)
    while total % width:
        width -= HDIM
    return width


def kernel(
    sections, split, wide, narrow,
    acts, norm_gain, final_gain, w_query, w_key, w_value, w_out, cache,
    updated, fresh,
    query_buf, key_buf, value_buf, out_buf, cache_buf, gain_buf, final_buf,
    gathered, normed, context, own_part, got_part, sent_rows, got_rows, total, slots, same_head,
    qkv_sem, out_sem, small_sem, act_send, act_recv, part_send, part_recv, mem_send, mem_recv,
):
    segment = lax.axis_index("segment")
    me = lax.axis_index("tensor")
    half = sections // 2
    root = half - 1
    decoder = segment >= half
    encoder = segment < half
    is_root = segment == root
    not_root = segment != root
    parts, local_rows, features = gathered.shape
    rows = parts * local_rows
    groups = query_buf.shape[0]
    blocks = out_buf.shape[0]

    def columns(j):
        return pl.ds(pl.multiple_of(j * wide, wide), wide)

    def load_qkv(which, source, target, j):
        return pltpu.make_async_copy(source.at[0, :, columns(j)], target.at[j], qkv_sem.at[which, j])

    def load_q(j):
        return load_qkv(0, w_query, query_buf, j)

    def load_k(j):
        return load_qkv(1, w_key, key_buf, j)

    def load_v(j):
        return load_qkv(2, w_value, value_buf, j)

    def load_out(c):
        return pltpu.make_async_copy(w_out.at[0, :, pl.ds(c * narrow, narrow)], out_buf.at[c], out_sem.at[c])

    own_acts = pltpu.make_async_copy(acts.at[0], gathered.at[me], small_sem.at[0])
    gain_copy = pltpu.make_async_copy(norm_gain, gain_buf, small_sem.at[1])
    final_copy = pltpu.make_async_copy(final_gain, final_buf, small_sem.at[2])
    cache_copy = pltpu.make_async_copy(cache.at[0], cache_buf, small_sem.at[3])

    barrier = pltpu.get_barrier_semaphore()
    for off in range(1, split):
        pl.semaphore_signal(barrier, inc=1, device_id={"tensor": lax.rem(me + off, split)}, device_id_type=MESH)

    @pl.when(is_root)
    def _():
        for s in range(half, sections):
            pl.semaphore_signal(barrier, inc=1, device_id={"segment": s}, device_id_type=MESH)

    @pl.when(decoder)
    def _():
        pl.semaphore_signal(barrier, inc=1, device_id={"segment": root}, device_id_type=MESH)

    own_acts.start()
    gain_copy.start()
    final_copy.start()

    @pl.when(encoder)
    def _():
        def begin(j, carry):
            load_q(j).start()
            load_k(j).start()
            load_v(j).start()
            return carry

        lax.fori_loop(0, groups, begin, 0)
        for c in range(blocks):
            load_out(c).start()

    @pl.when(decoder)
    def _():
        cache_copy.start()

        def begin(j, carry):
            load_q(j).start()
            return carry

        lax.fori_loop(0, groups, begin, 0)
        for c in range(blocks):
            load_out(c).start()

        def begin_pair(j, carry):
            load_k(j).start()
            load_v(j).start()
            return carry

        lax.fori_loop(0, groups, begin_pair, 0)

    @pl.when(is_root)
    def _():
        pl.semaphore_wait(barrier, split - 1 + sections - half)

    @pl.when(decoder)
    def _():
        pl.semaphore_wait(barrier, split)

    @pl.when(encoder & not_root)
    def _():
        pl.semaphore_wait(barrier, split - 1)

    def send_acts(off):
        return pltpu.make_async_remote_copy(
            src_ref=acts.at[0],
            dst_ref=gathered.at[me],
            send_sem=act_send.at[off - 1],
            recv_sem=act_recv.at[off - 1],
            device_id={"tensor": lax.rem(me + off, split)},
            device_id_type=MESH,
        )

    def send_all_rows(off, c):
        return pltpu.make_async_remote_copy(
            src_ref=own_part.at[c],
            dst_ref=got_part.at[off - 1, c],
            send_sem=part_send.at[off - 1, c],
            recv_sem=part_recv.at[off - 1, c],
            device_id={"tensor": lax.rem(me + off, split)},
            device_id_type=MESH,
        )

    def send_their_rows(off, c):
        peer = lax.rem(me + off, split)
        return pltpu.make_async_remote_copy(
            src_ref=own_part.at[c, peer],
            dst_ref=got_part.at[off - 1, c, peer],
            send_sem=part_send.at[off - 1, c],
            recv_sem=part_recv.at[off - 1, c],
            device_id={"tensor": peer},
            device_id_type=MESH,
        )

    def send_memory(s, c):
        return pltpu.make_async_remote_copy(
            src_ref=sent_rows.at[c],
            dst_ref=got_rows.at[c],
            send_sem=mem_send.at[s - half, c],
            recv_sem=mem_recv.at[c],
            device_id={"segment": s},
            device_id_type=MESH,
        )

    for off in range(1, split):
        send_acts(off).start()
    own_acts.wait()
    gain_copy.wait()
    final_copy.wait()
    for off in range(1, split):
        send_acts(off).wait_recv()

    tokens = gathered[...].reshape(rows, features).astype(F32)
    scale = lax.rsqrt(jnp.mean(tokens * tokens, axis=-1, keepdims=True) + EPSILON)
    normed[...] = (tokens * scale * gain_buf[...]).astype(BF16)

    which_row = lax.broadcasted_iota(jnp.int32, same_head.shape, 0) < rows
    which_column = lax.broadcasted_iota(jnp.int32, same_head.shape, 1) < rows
    same_head[...] = jnp.where(which_row == which_column, 1.0, 0.0).astype(BF16)

    def attend(queries, keys, values):
        blank = jnp.zeros((rows, HDIM), BF16)
        pairs = wide // (2 * HDIM)

        def spread(source, p):
            first = source[:, 2 * p * HDIM : (2 * p + 1) * HDIM]
            second = source[:, (2 * p + 1) * HDIM : (2 * p + 2) * HDIM]
            return jnp.concatenate(
                [jnp.concatenate([first, blank], axis=1), jnp.concatenate([blank, second], axis=1)], axis=0
            )

        scores = [
            lax.dot_general(
                queries[:, 2 * p * HDIM : (2 * p + 2) * HDIM], spread(keys, p),
                (((1,), (1,)), ((), ())), preferred_element_type=F32,
            )
            for p in range(pairs)
        ]
        weights = [jnp.minimum(jnp.exp(score), LARGEST) for score in scores]
        ones = same_head[...]
        sums = [jnp.dot(weight.astype(BF16), ones, preferred_element_type=F32) for weight in weights]
        probs = [(weight / total_of).astype(BF16) for weight, total_of in zip(weights, sums)]
        results = [
            jnp.dot(probs[p], spread(values, p), preferred_element_type=F32).astype(BF16) for p in range(pairs)
        ]
        return jnp.concatenate(results, axis=1)

    def attend_slot(slot, j):
        context[:, columns(j)] = attend(slots[slot, 0], slots[slot, 1], slots[slot, 2])

    def own_group(slot, j):
        source = normed[...]
        for which, weights in ((0, query_buf), (1, key_buf), (2, value_buf)):
            made = jnp.dot(source, weights[j], preferred_element_type=F32).astype(BF16)
            slots[slot, which] = made
            if which > 0:
                fresh[0, which - 1, :, columns(j)] = made

    def cached_group(slot, j):
        made = jnp.dot(normed[...], query_buf[j], preferred_element_type=F32).astype(BF16)
        slots[slot, 0] = made
        slots[slot, 1] = cache_buf[0, :, columns(j)]
        slots[slot, 2] = cache_buf[1, :, columns(j)]

    def pipelined(wait, make):
        wait(0)
        make(0, 0)

        def pair(i, carry):
            j = 2 * i + 1
            wait(j)
            attend_slot(0, j - 1)
            make(1, j)
            wait(j + 1)
            attend_slot(1, j)
            make(0, j + 1)
            return carry

        lax.fori_loop(0, (groups - 1) // 2, pair, 0)
        if groups % 2 == 0:
            wait(groups - 1)
            attend_slot(0, groups - 2)
            make(1, groups - 1)
        attend_slot((groups - 1) % 2, groups - 1)

    @pl.when(encoder)
    def _():
        def wait(j):
            load_q(j).wait()
            load_k(j).wait()
            load_v(j).wait()

        pipelined(wait, own_group)

    @pl.when(decoder)
    def _():
        cache_copy.wait()
        pipelined(lambda j: load_q(j).wait(), cached_group)

    def project(c):
        load_out(c).wait()
        made = jnp.dot(context[...], out_buf[c], preferred_element_type=F32).astype(BF16)
        own_part[c] = made.reshape(parts, local_rows, narrow)

        @pl.when(is_root)
        def _():
            for off in range(1, split):
                send_all_rows(off, c).start()

        @pl.when(not_root)
        def _():
            for off in range(1, split):
                send_their_rows(off, c).start()

    def combine(c):
        cols = slice(c * narrow, (c + 1) * narrow)

        @pl.when(is_root)
        def _():
            for off in range(1, split):
                send_all_rows(off, c).wait_recv()
            branch = own_part[c].astype(F32)
            for off in range(1, split):
                branch = branch + got_part[off - 1, c].astype(F32)
            sent_rows[c] = (gathered[:, :, cols].astype(F32) + branch).astype(BF16)
            for s in range(half, sections):
                send_memory(s, c).start()
            updated[0, :, cols] = sent_rows[c, me]

        @pl.when(not_root)
        def _():
            for off in range(1, split):
                send_their_rows(off, c).wait_recv()
            branch = own_part[c, me].astype(F32)
            for off in range(1, split):
                branch = branch + got_part[off - 1, c, me].astype(F32)
            updated[0, :, cols] = (gathered[me, :, cols].astype(F32) + branch).astype(BF16)

    lag = min(2, blocks - 1)
    for c in range(blocks):
        project(c)
        if c >= lag:
            combine(c - lag)
    for c in range(blocks - lag, blocks):
        combine(c)

    @pl.when(decoder)
    def _():
        def arrive(j, carry):
            load_k(j).wait()
            load_v(j).wait()
            return carry

        lax.fori_loop(0, groups, arrive, 0)
        squares = jnp.zeros((rows, 1), F32)
        for c in range(blocks):
            cols = slice(c * narrow, (c + 1) * narrow)
            send_memory(half, c).wait_recv()
            memory = got_rows[c].reshape(rows, narrow).astype(F32)
            squares = squares + jnp.sum(memory * memory, axis=-1, keepdims=True)
            source = (memory * final_buf[:, cols]).astype(BF16)
            last = c == blocks - 1
            if last:
                scale = lax.rsqrt(squares * (1.0 / features) + EPSILON)

            def group(j, carry):
                for which, weights in ((0, key_buf), (1, value_buf)):
                    term = jnp.dot(source, weights[j, cols, :], preferred_element_type=F32)
                    if c > 0:
                        term = term + total[which, j]
                    if last:
                        fresh[0, which, :, columns(j)] = (term * scale).astype(BF16)
                    else:
                        total[which, j] = term
                return carry

            lax.fori_loop(0, groups, group, 0, unroll=True)

    for off in range(1, split):
        send_acts(off).wait_send()

    @pl.when(is_root)
    def _():
        for c in range(blocks):
            for off in range(1, split):
                send_all_rows(off, c).wait_send()
            for s in range(half, sections):
                send_memory(s, c).wait_send()

    @pl.when(not_root)
    def _():
        for c in range(blocks):
            for off in range(1, split):
                send_their_rows(off, c).wait_send()


def solution(mesh):
    sections, split = mesh.shape["segment"], mesh.shape["tensor"]

    def on_device(acts, norm_gain, final_gain, w_query, w_key, w_value, w_out, cache):
        local_rows, features = acts.shape[1:]
        inner = w_query.shape[2]
        rows = split * local_rows
        wide = largest(inner, 1024)
        narrow = largest(features, 256)
        groups, blocks = inner // wide, features // narrow
        dma = pltpu.SemaphoreType.DMA
        return pl.pallas_call(
            functools.partial(kernel, sections, split, wide, narrow),
            out_shape=(pltpu.VMEM(acts.shape, BF16), pltpu.VMEM(cache.shape, BF16)),
            in_specs=[pl.BlockSpec(memory_space=pltpu.HBM)] * 8,
            out_specs=(pl.BlockSpec(memory_space=pltpu.VMEM), pl.BlockSpec(memory_space=pltpu.VMEM)),
            scratch_shapes=[
                pltpu.VMEM((groups, features, wide), BF16),
                pltpu.VMEM((groups, features, wide), BF16),
                pltpu.VMEM((groups, features, wide), BF16),
                pltpu.VMEM((blocks, inner, narrow), BF16),
                pltpu.VMEM((2, rows, inner), BF16),
                pltpu.VMEM((1, features), F32),
                pltpu.VMEM((1, features), F32),
                pltpu.VMEM((split, local_rows, features), BF16),
                pltpu.VMEM((rows, features), BF16),
                pltpu.VMEM((rows, inner), BF16),
                pltpu.VMEM((blocks, split, local_rows, narrow), BF16),
                pltpu.VMEM((split - 1, blocks, split, local_rows, narrow), BF16),
                pltpu.VMEM((blocks, split, local_rows, narrow), BF16),
                pltpu.VMEM((blocks, split, local_rows, narrow), BF16),
                pltpu.VMEM((2, groups, rows, wide), F32),
                pltpu.VMEM((2, 3, rows, wide), BF16),
                pltpu.VMEM((2 * rows, 2 * rows), BF16),
                dma((3, groups)),
                dma((blocks,)),
                dma((4,)),
                dma((split - 1,)),
                dma((split - 1,)),
                dma((split - 1, blocks)),
                dma((split - 1, blocks)),
                dma((sections - sections // 2, blocks)),
                dma((blocks,)),
            ],
            compiler_params=pltpu.CompilerParams(
                collective_id=0, has_side_effects=True, vmem_limit_bytes=58 * 1024 * 1024
            ),
        )(acts, norm_gain, final_gain.reshape(1, features), w_query, w_key, w_value, w_out, cache)

    placed = (
        P("segment", ("dp", "tensor"), None),
        P("segment", None),
        P(),
        P("segment", None, "tensor"),
        P("segment", None, "tensor"),
        P("segment", None, "tensor"),
        P("segment", "tensor", None),
        P("segment", None, "dp", "tensor"),
    )
    return jax.shard_map(
        on_device,
        mesh=mesh,
        in_specs=placed,
        out_specs=(P("segment", ("dp", "tensor"), None), P("segment", None, "dp", "tensor")),
        check_vma=False,
    )
```
